32 devices in a mesh: energy: 16 (over z, y, x), space: 2 (over core).
Axes of the slice: x: 2, y: 2, z: 4, core: 2. Of those that a mesh axis runs over, the one named last changes fastest.
Arguments:
- green0: bfloat16 [128, 2, 2, 192, 192], P('energy', 'space'), may hold values from -1.5 to 1
- coupling: bfloat16 [2, 192, 192], P('space'), may hold values from -0.375 to 0.375
- pattern: int32 [2, 4, 4], P('space'), may hold values 0 or 1
- broaden: bfloat16 [128, 2, 192, 192], P('energy', 'space'), may hold values from -0.5 to 1.5
- screened: float32 [128, 2, 192, 384], P(None, 'space', 'energy'), may hold values from -6 to 6
- order: int32 [192], replicated, may hold values from 0 to 191, each once
Outputs:
- sigma: float32 [128, 2, 192, 384], P('energy', 'space')
The draws below stay inside these ranges and needn't reach their ends.
All inputs are finite; a program needn't handle non-finite values. No bound on the sum of `pattern` on one device may be relied on, other than what follows from the above.
Results may differ from the reference program's by a relative error of at most 0.0059.
Values may be sent and summed in bfloat16 or wider, within the bound.
A program may use at most 128 MiB of HBM per device.

```python
import math
import jax
import jax.numpy as jnp
from jax import lax

BS = 192
TB = 4
NE = 128
NB = 2


def draw_green0(key, part):
    key_list = jax.random.split(key, 3)
    full_shape = (NE, NB, 2, BS, BS)
    rough_part = jnp.clip(jax.random.normal(key_list[0], full_shape, jnp.float32), -4.0, 4.0)
    symmetric = (rough_part + jnp.swapaxes(rough_part, -1, -2)) * (0.3 / math.sqrt(2.0 * BS))
    diag_real = jax.random.uniform(key_list[1], (NE, NB, 1, BS), jnp.float32, -1.0, 1.0)
    diag_imag = jax.random.uniform(key_list[2], (NE, NB, 1, BS), jnp.float32, -1.5, -0.4)
    diag_values = jnp.concatenate([diag_real, diag_imag], axis=2)
    diagonal_ones = jnp.eye(BS, dtype=jnp.float32)
    return (symmetric * (1.0 - diagonal_ones) + diag_values[..., None] * diagonal_ones).astype(jnp.bfloat16)


def draw_broaden(key, part):
    key_list = jax.random.split(key, 2)
    full_shape = (NE, NB, BS, BS)
    rough_part = jnp.clip(jax.random.normal(key_list[0], full_shape, jnp.float32), -4.0, 4.0)
    symmetric = (rough_part + jnp.swapaxes(rough_part, -1, -2)) * (0.3 / math.sqrt(2.0 * BS))
    diag_values = jax.random.uniform(key_list[1], (NE, NB, BS), jnp.float32, 0.2, 1.5)
    diagonal_ones = jnp.eye(BS, dtype=jnp.float32)
    return (symmetric * (1.0 - diagonal_ones) + diag_values[..., None] * diagonal_ones).astype(jnp.bfloat16)


def plant(drawn, own_key, least, high):
    shape = drawn.shape
    spot = [jax.random.randint(jax.random.fold_in(own_key, axis), (), 0, shape[axis]) for axis in range(len(shape))]
    drawn = drawn.at[tuple(spot)].set(least)
    longest = shape.index(max(shape))
    spot[longest] = (spot[longest] + 1) % shape[longest]
    return drawn.at[tuple(spot)].set(high)


def levels(own_key, dims, cuts, smallest, high):
    gain, own = 1.0, jax.random.fold_in(own_key, 6)
    for dim, blocks in cuts:
        heights = jnp.exp(jax.random.uniform(jax.random.fold_in(own, dim), (blocks,), jnp.float32, smallest / len(cuts), high / len(cuts)))
        gain = gain * jnp.repeat(heights, dims[dim] // blocks).reshape([-1 if axis == dim else 1 for axis in range(len(dims))])
    return gain


def normal_values(stream_key, shape, width, reach, cuts=(), kind=jnp.bfloat16):
    result = width * jax.random.normal(stream_key, shape, jnp.float32)
    if cuts:
        result = result * levels(stream_key, shape, cuts, -0.22, 0.18)
    return jnp.clip(result, -reach, reach).astype(kind)


def setup_inputs(seed: int = 0) -> dict:
    streams_of = jax.random.split(jax.random.key(seed), 7)
    return {
        "green0": draw_green0(jax.random.fold_in(streams_of[6], 71), 0),
        "coupling": normal_values(streams_of[1], (NB, BS, BS), (5 * BS // 4) ** -0.5, 0.375, ((0, 2),)),
        "pattern": plant((jax.random.randint(streams_of[2], (NB, TB, TB), 0, 4) < 3).astype(jnp.int32), jax.random.fold_in(streams_of[2], 1), 0, 1),
        "broaden": draw_broaden(jax.random.fold_in(streams_of[6], 71), 0),
        "screened": normal_values(streams_of[4], (NE, NB, BS, 2 * BS), 1.0, 6.0, ((1, 2), (2, 16)), jnp.float32),
        "order": jax.random.permutation(streams_of[5], BS).astype(jnp.int32),
    }


def to_half(values):
    return values.astype(jnp.bfloat16)

def flip_last(values):
    return jnp.swapaxes(values, -1, -2)

def complex_product(left_op, right_op):
    left_op = left_op.astype(jnp.float32)
    right_op = right_op.astype(jnp.float32)

    def matmul(first_op, second):
        return jnp.einsum('...ij,...jk->...ik', first_op, second)
    real_part = matmul(left_op[..., 0, :, :], right_op[..., 0, :, :]) - matmul(left_op[..., 1, :, :], right_op[..., 1, :, :])
    imag_part = matmul(left_op[..., 0, :, :], right_op[..., 1, :, :]) + matmul(left_op[..., 1, :, :], right_op[..., 0, :, :])
    return jnp.stack([real_part, imag_part], axis=-3)

def reference(green0, coupling, pattern, broaden, screened, order):
    tile_size = BS // TB
    spread = jnp.repeat(jnp.repeat(pattern, tile_size, axis=1), tile_size, axis=2)
    couple = coupling * spread.astype(jnp.bfloat16)
    couple_f = couple.astype(jnp.float32)

    def one_energy(items):
        green_cell, gamma_cell = items
        green_f = green_cell.astype(jnp.float32)
        factor = to_half(jnp.einsum('bcij,bjk->bcik', green_f, couple_f))
        added_term = to_half(jnp.einsum('bcij,bjk->bcik', flip_last(factor).astype(jnp.float32), couple_f))

        def left_step(carried, pieces):
            green_b, factor_b = pieces
            left_b = green_b.astype(jnp.float32) + complex_product(to_half(complex_product(factor_b, carried)), flip_last(factor_b))
            return (to_half(left_b), left_b)
        unused, left_part = lax.scan(left_step, green_cell[0], (green_cell, factor))

        def right_step(passed, pieces):
            green_b, factor_b, added_b = pieces
            right_b = green_b.astype(jnp.float32) + complex_product(to_half(complex_product(green_b, passed)), green_b)
            moved = to_half(complex_product(flip_last(factor_b), passed))
            passed_next = to_half(complex_product(moved, factor_b) + added_b.astype(jnp.float32))
            return (passed_next, right_b)
        unused, right_part = lax.scan(right_step, jnp.zeros_like(green_cell[0]), (green_cell, factor, added_term), reverse=True)
        full_green = to_half(left_part + right_part - green_f).astype(jnp.float32)
        weighted = to_half(jnp.einsum('bcij,bjk->bcik', full_green, gamma_cell.astype(jnp.float32))).astype(jnp.float32)

        def outer_product(first_op, second):
            return jnp.einsum('bij,bkj->bik', first_op, second)
        real_part = outer_product(weighted[:, 0], full_green[:, 1]) - outer_product(weighted[:, 1], full_green[:, 0])
        imag_part = outer_product(weighted[:, 0], full_green[:, 0]) + outer_product(weighted[:, 1], full_green[:, 1])
        return jnp.concatenate([real_part, imag_part], axis=-1)
    lesser = lax.map(one_energy, (green0, broaden))
    slotted = jnp.take(lesser, order, axis=2)

    def convolve(items):
        values, kernel = items
        value_c = values[..., :BS] + 1j * values[..., BS:]
        kernel_c = kernel[..., :BS] + 1j * kernel[..., BS:]
        mixed = jnp.fft.ifft(jnp.fft.fft(value_c, axis=0) * jnp.fft.fft(kernel_c, axis=0), axis=0) * (1j / math.sqrt(NE))
        return jnp.concatenate([jnp.real(mixed), jnp.imag(mixed)], axis=-1)
    sigma_slot = lax.map(convolve, (jnp.moveaxis(slotted, 1, 0), jnp.moveaxis(screened, 1, 0)))
    sigma_slot = jnp.moveaxis(sigma_slot, 0, 1)
    sigma_rows = jnp.zeros_like(sigma_slot).at[:, :, order, :].set(sigma_slot)
    return sigma_rows.astype(jnp.float32)
```

```python
import functools
import math

import jax
import jax.numpy as jnp
import numpy as np
from jax import lax
from jax.experimental import pallas as pl
from jax.experimental.pallas import tpu as pltpu
from jax.sharding import PartitionSpec as P

F32 = jnp.float32
BF16 = jnp.bfloat16
PLAIN = ((1,), (0,))
LAST = ((1,), (1,))
FIRST = ((0,), (0,))


def dot(a, b, dims=PLAIN):
    return lax.dot_general(a, b, (dims, ((), ())), preferred_element_type=F32)


def complex_dot(left, right_re, right_im, dims=PLAIN):
    rows = left.shape[0] // 2
    with_re = dot(left, right_re, dims)
    with_im = dot(left, right_im, dims)
    return (with_re[:rows] - with_im[rows:], with_im[:rows] + with_re[rows:])


def stack(pair):
    return jnp.concatenate(pair, axis=0)


def born_kernel(first_ref, green_ref, couple_ref, send_ref, mult_ref, base_ref):
    green = green_ref[0]
    rows = green.shape[0] // 2
    couple = couple_ref[...]
    factor = dot(green, couple).astype(BF16)

    @pl.when(first_ref[0] == 1)
    def _():
        moved = stack(complex_dot(factor, green[:rows], green[rows:])).astype(BF16)
        image = green.astype(F32) + stack(complex_dot(moved, factor[:rows], factor[rows:], LAST))
        base_ref[0] = image
        send_ref[0] = image.astype(BF16)
        mult_ref[0] = green

    @pl.when(first_ref[0] == 0)
    def _():
        base_ref[0] = green.astype(F32)
        send_ref[0, :rows] = dot(factor[:rows], couple, FIRST).astype(BF16)
        send_ref[0, rows:] = dot(factor[rows:], couple, FIRST).astype(BF16)
        mult_ref[0] = factor


def lesser_kernel(
    owners, first_ref, mult_ref, got_ref, base_ref, gamma_ref, pick_ref, mix_ref, out_ref, full_s, slots_s
):
    energy = pl.program_id(0)
    mult = mult_ref[0]
    rows = mult.shape[0] // 2
    got = got_ref[0]
    moved = stack(complex_dot(mult, got[:rows], got[rows:])).astype(BF16)

    @pl.when(first_ref[0] == 1)
    def _():
        full_s[...] = (base_ref[0] + stack(complex_dot(moved, mult[:rows], mult[rows:]))).astype(BF16)

    @pl.when(first_ref[0] == 0)
    def _():
        full_s[...] = (base_ref[0] + stack(complex_dot(moved, mult[:rows], mult[rows:], LAST))).astype(BF16)

    full = full_s[...]
    weighted = dot(full, gamma_ref[0]).astype(BF16)
    pick = pick_ref[...]
    weighted = stack((dot(pick, weighted[:rows]), dot(pick, weighted[rows:]))).astype(BF16)
    with_re = dot(weighted, full[:rows], LAST)
    with_im = dot(weighted, full[rows:], LAST)
    lesser = jnp.concatenate(
        [with_im[:rows] - with_re[rows:], with_re[:rows] + with_im[rows:]], axis=1
    ).astype(BF16)
    share = rows // owners
    for r in range(share):
        slots_s[r, pl.ds(pl.multiple_of(energy * owners, owners), owners), :] = lesser[
            r * owners : (r + 1) * owners
        ]

    @pl.when(energy == pl.num_programs(0) - 1)
    def _():
        mix = mix_ref[...]
        width = lesser.shape[1]
        for r in range(share):
            out_ref[:, r * width : (r + 1) * width] = dot(mix, slots_s[r]).astype(BF16)


def times_i(values):
    half = values.shape[1] // 2
    return jnp.concatenate([-values[:, half:], values[:, :half]], axis=1)


def transform(table, upper, lower):
    both = dot(table, jnp.concatenate([upper, lower], axis=0).astype(BF16))
    points = upper.shape[0]
    return both[:points] + both[points:]


def screened_kernel(scale, table_ref, values_ref, out_ref):
    width = values_ref.shape[2]
    for r in range(values_ref.shape[1]):
        values = values_ref[:, r, :]
        out_ref[:, r * width : (r + 1) * width] = (
            transform(table_ref[...], values, times_i(values)) * scale
        )


def convolve_kernel(table_ref, values_ref, kernel_ref, out_ref):
    values = values_ref[...].astype(F32)
    kernel = kernel_ref[...]
    half = kernel.shape[1] // 2
    table = table_ref[...]
    spectrum = transform(table, values, times_i(values))
    kernel_re = jnp.concatenate([kernel[:, :half], kernel[:, :half]], axis=1)
    kernel_im = jnp.concatenate([kernel[:, half:], kernel[:, half:]], axis=1)
    product = spectrum * kernel_re + times_i(spectrum) * kernel_im
    out_ref[...] = transform(table, times_i(product), product).astype(BF16)


def restore_kernel(owners, values_ref, unmix_ref, place_ref, out_ref, slots_s):
    energy = pl.program_id(0)
    width = out_ref.shape[2]
    share = out_ref.shape[1] // owners

    @pl.when(energy == 0)
    def _():
        unmix = unmix_ref[...]
        for r in range(share):
            slots_s[r] = dot(unmix, values_ref[:, r * width : (r + 1) * width]).astype(BF16)

    at = pl.ds(pl.multiple_of(energy * owners, owners), owners)
    ordered = jnp.concatenate([slots_s[r, at, :] for r in range(share)], axis=0)
    out_ref[0] = dot(place_ref[...], ordered)


def whole(shape):
    return pl.BlockSpec(shape, lambda e: (0,) * len(shape))


def per_energy(*shape):
    return pl.BlockSpec((1,) + shape, lambda e: (e,) + (0,) * len(shape))


def params():
    return pltpu.CompilerParams(dimension_semantics=("arbitrary",))


def cost(flops, moved):
    return pl.CostEstimate(flops=int(flops), bytes_accessed=int(moved), transcendentals=0)


def on_device(owners, green0, coupling, pattern, broaden, screened, order):
    here = green0.shape[0]
    size = green0.shape[-1]
    points = screened.shape[0]
    share = size // owners
    width = 2 * size
    flat = share * width
    green = green0.reshape(here, 2 * size, size)
    gamma = broaden.reshape(here, size, size)
    tile_size = size // pattern.shape[-1]
    spread = jnp.repeat(jnp.repeat(pattern[0], tile_size, axis=0), tile_size, axis=1)
    couple = coupling[0] * spread.astype(BF16)
    first = (lax.axis_index("space") == 0).astype(jnp.int32).reshape(1)
    by_row = order.reshape(owners, share).T.reshape(-1)
    ids = jnp.arange(size, dtype=jnp.int32)
    pick = (by_row[:, None] == ids[None, :]).astype(BF16)
    place = (by_row[None, :] == ids[:, None]).astype(BF16)

    ticks = np.arange(points)
    angles = (ticks[:, None] * ticks[None, :] % points) * (2.0 * math.pi / points)
    exact = np.concatenate([np.cos(angles), -np.sin(angles)], axis=1)
    high = exact.astype(BF16)
    low = (exact - high.astype(np.float64)).astype(BF16)
    table = jnp.asarray(np.concatenate([high, low], axis=0))
    where = np.arange(here * owners)
    source = (where % here) * owners + where // here
    mix_np = (source[:, None] == where[None, :]).astype(np.float32)
    mix = jnp.asarray(mix_np.astype(BF16))
    unmix = jnp.asarray(mix_np.T.astype(BF16))

    kernel = pl.pallas_call(
        functools.partial(screened_kernel, 1.0 / (points * math.sqrt(points))),
        out_shape=jax.ShapeDtypeStruct((points, flat), F32),
        cost_estimate=cost(8.0 * points * points * flat, 8 * points * flat),
        name="screened_spectrum",
    )(table, screened.reshape(points, share, width))

    smem = pl.BlockSpec(memory_space=pltpu.SMEM)
    cell = (2 * size, size)
    work = 2.0 * here * size**3
    send, mult, base = pl.pallas_call(
        born_kernel,
        grid=(here,),
        in_specs=[smem, per_energy(*cell), whole((size, size))],
        out_specs=[per_energy(*cell)] * 3,
        out_shape=[
            jax.ShapeDtypeStruct((here,) + cell, BF16),
            jax.ShapeDtypeStruct((here,) + cell, BF16),
            jax.ShapeDtypeStruct((here,) + cell, F32),
        ],
        compiler_params=params(),
        cost_estimate=cost(10 * work, 10 * here * 2 * size * size),
        name="born",
    )(first, green, couple)
    got = lax.ppermute(send, "space", [(0, 1), (1, 0)])
    mixed = pl.pallas_call(
        functools.partial(lesser_kernel, owners),
        grid=(here,),
        in_specs=[
            smem,
            per_energy(*cell),
            per_energy(*cell),
            per_energy(*cell),
            per_energy(size, size),
            whole((size, size)),
            whole((here * owners, here * owners)),
        ],
        out_specs=whole((here * owners, flat)),
        out_shape=jax.ShapeDtypeStruct((here * owners, flat), BF16),
        scratch_shapes=[
            pltpu.VMEM(cell, BF16),
            pltpu.VMEM((share, here * owners, width), BF16),
        ],
        compiler_params=params(),
        cost_estimate=cost(16 * work, 14 * here * 2 * size * size),
        name="lesser",
    )(first, mult, got, base, gamma, pick, mix)
    gathered = lax.all_to_all(mixed, "energy", split_axis=0, concat_axis=0, tiled=True)
    column = pl.BlockSpec((points, width), lambda r: (0, r))
    sigma = pl.pallas_call(
        convolve_kernel,
        grid=(share,),
        in_specs=[whole((2 * points, 2 * points)), column, column],
        out_specs=column,
        out_shape=jax.ShapeDtypeStruct((points, flat), BF16),
        compiler_params=params(),
        cost_estimate=cost(16.0 * points * points * flat, 8 * points * flat),
        name="convolve",
    )(table, gathered, kernel)
    returned = lax.all_to_all(sigma, "energy", split_axis=0, concat_axis=0, tiled=True)
    out = pl.pallas_call(
        functools.partial(restore_kernel, owners),
        grid=(here,),
        in_specs=[
            whole((here * owners, flat)),
            whole((here * owners, here * owners)),
            whole((size, size)),
        ],
        out_specs=per_energy(size, width),
        out_shape=jax.ShapeDtypeStruct((here, size, width), F32),
        scratch_shapes=[pltpu.VMEM((share, here * owners, width), BF16)],
        compiler_params=params(),
        cost_estimate=cost(4 * work, 6 * points * flat),
        name="restore",
    )(returned, unmix, place)
    return out[:, None]


def solution(mesh):
    return jax.shard_map(
        functools.partial(on_device, mesh.shape["energy"]),
        mesh=mesh,
        in_specs=(
            P("energy", "space", None, None, None),
            P("space", None, None),
            P("space", None, None),
            P("energy", "space", None, None),
            P(None, "space", "energy", None),
            P(),
        ),
        out_specs=P("energy", "space", None, None),
        check_vma=False,
    )
```

```python
import functools
import math

import jax
import jax.numpy as jnp
import numpy as np
from jax import lax
from jax.experimental import pallas as pl
from jax.experimental.pallas import tpu as pltpu
from jax.sharding import PartitionSpec as P

F32 = jnp.float32
BF16 = jnp.bfloat16
PLAIN = ((1,), (0,))
LAST = ((1,), (1,))
FIRST = ((0,), (0,))


def dot(a, b, dims=PLAIN):
    return lax.dot_general(a, b, (dims, ((), ())), preferred_element_type=F32)


def complex_dot(left, right_re, right_im, dims=PLAIN):
    rows = left.shape[0] // 2
    with_re = dot(left, right_re, dims)
    with_im = dot(left, right_im, dims)
    return (with_re[:rows] - with_im[rows:], with_im[:rows] + with_re[rows:])


def stack(pair):
    return jnp.concatenate(pair, axis=0)


def born_kernel(first_ref, green_ref, couple_ref, send_ref, mult_ref, base_ref):
    green = green_ref[0]
    rows = green.shape[0] // 2
    couple = couple_ref[...]
    factor = dot(green, couple).astype(BF16)

    @pl.when(first_ref[0] == 1)
    def _():
        moved = stack(complex_dot(factor, green[:rows], green[rows:])).astype(BF16)
        image = green.astype(F32) + stack(complex_dot(moved, factor[:rows], factor[rows:], LAST))
        base_ref[0] = image
        send_ref[0] = jnp.concatenate([image[:rows], image[rows:]], axis=1).astype(BF16)
        mult_ref[0] = green

    @pl.when(first_ref[0] == 0)
    def _():
        base_ref[0] = green.astype(F32)
        added = [dot(factor[:rows], couple, FIRST), dot(factor[rows:], couple, FIRST)]
        send_ref[0] = jnp.concatenate(added, axis=1).astype(BF16)
        mult_ref[0] = factor


def lesser_kernel(
    owners, first_ref, mult_ref, got_ref, base_ref, gamma_ref, pick_ref, mix_ref, out_ref, full_s, slots_s
):
    energy = pl.program_id(0)
    mult = mult_ref[0]
    rows = mult.shape[0] // 2
    got = got_ref[0]
    moved = stack(complex_dot(mult, got[:, :rows], got[:, rows:])).astype(BF16)

    @pl.when(first_ref[0] == 1)
    def _():
        full_s[...] = (base_ref[0] + stack(complex_dot(moved, mult[:rows], mult[rows:]))).astype(BF16)

    @pl.when(first_ref[0] == 0)
    def _():
        full_s[...] = (base_ref[0] + stack(complex_dot(moved, mult[:rows], mult[rows:], LAST))).astype(BF16)

    full = full_s[...]
    weighted = dot(full, gamma_ref[0]).astype(BF16)
    pick = pick_ref[...]
    weighted = stack((dot(pick, weighted[:rows]), dot(pick, weighted[rows:]))).astype(BF16)
    with_re = dot(weighted, full[:rows], LAST)
    with_im = dot(weighted, full[rows:], LAST)
    lesser = jnp.concatenate(
        [with_im[:rows] - with_re[rows:], with_re[:rows] + with_im[rows:]], axis=1
    ).astype(BF16)
    share = rows // owners
    for r in range(share):
        slots_s[r, pl.ds(pl.multiple_of(energy * owners, owners), owners), :] = lesser[
            r * owners : (r + 1) * owners
        ]

    @pl.when(energy == pl.num_programs(0) - 1)
    def _():
        mix = mix_ref[...]
        width = lesser.shape[1]
        for r in range(share):
            out_ref[:, r * width : (r + 1) * width] = dot(mix, slots_s[r]).astype(BF16)


def times_i(values):
    half = values.shape[1] // 2
    return jnp.concatenate([-values[:, half:], values[:, :half]], axis=1)


def transform(table, upper, lower):
    both = dot(table, jnp.concatenate([upper, lower], axis=0).astype(BF16))
    points = upper.shape[0]
    return both[:points] + both[points:]


def exchange_kernel(
    owners,
    groups,
    scale,
    table_ref,
    mixed_ref,
    screened_ref,
    back_ref,
    screened_s,
    spectrum_s,
    got_s,
    sigma_s,
    away_sent,
    away_landed,
    back_sent,
    back_landed,
    own_sem,
):
    me = lax.axis_index("energy")
    points, share, width = screened_s.shape
    each = share // groups
    span = each * width

    def columns(g):
        return pl.ds(g * span, span)

    def away(g, k):
        peer = lax.rem(me + k, owners)
        return pltpu.make_async_remote_copy(
            src_ref=mixed_ref.at[peer, :, columns(g)],
            dst_ref=got_s.at[me, :, columns(g)],
            send_sem=away_sent.at[g, k - 1],
            recv_sem=away_landed.at[g, k - 1],
            device_id={"energy": peer},
            device_id_type=pl.DeviceIdType.MESH,
        )

    def back(g, k):
        peer = lax.rem(me + k, owners)
        return pltpu.make_async_remote_copy(
            src_ref=sigma_s.at[peer, :, columns(g)],
            dst_ref=back_ref.at[me, :, columns(g)],
            send_sem=back_sent.at[g, k - 1],
            recv_sem=back_landed.at[g, k - 1],
            device_id={"energy": peer},
            device_id_type=pl.DeviceIdType.MESH,
        )

    def for_peers(action):
        lax.fori_loop(1, owners, lambda k, c: (action(k), c)[1], 0)

    barrier = pltpu.get_barrier_semaphore()
    for_peers(
        lambda k: pl.semaphore_signal(
            barrier,
            inc=1,
            device_id={"energy": lax.rem(me + k, owners)},
            device_id_type=pl.DeviceIdType.MESH,
        )
    )
    load = pltpu.make_async_copy(screened_ref, screened_s, own_sem.at[0])
    load.start()
    keep = pltpu.make_async_copy(mixed_ref.at[me], got_s.at[me], own_sem.at[1])
    keep.start()
    pl.semaphore_wait(barrier, owners - 1)
    for g in range(groups):
        for_peers(lambda k: away(g, k).start())
    load.wait()
    table = table_ref[...]
    for r in range(share):
        values = screened_s[:, r, :]
        spectrum_s[:, r * width : (r + 1) * width] = transform(table, values, times_i(values)) * scale
    keep.wait()
    half = width // 2
    owns = []
    for g in range(groups):
        for_peers(lambda k: away(g, k).wait_recv())
        for r in range(g * each, (g + 1) * each):
            at = slice(r * width, (r + 1) * width)
            values = got_s[:, :, at].astype(F32).reshape(points, width)
            kernel = spectrum_s[:, at]
            spectrum = transform(table, values, times_i(values))
            kernel_re = jnp.concatenate([kernel[:, :half], kernel[:, :half]], axis=1)
            kernel_im = jnp.concatenate([kernel[:, half:], kernel[:, half:]], axis=1)
            product = spectrum * kernel_re + times_i(spectrum) * kernel_im
            result = transform(table, times_i(product), product)
            sigma_s[:, :, at] = result.reshape(owners, points // owners, width).astype(BF16)
        for_peers(lambda k: back(g, k).start())
        own = pltpu.make_async_copy(
            sigma_s.at[me, :, columns(g)], back_ref.at[me, :, columns(g)], own_sem.at[2 + g]
        )
        own.start()
        owns.append(own)
    for g in range(groups):
        owns[g].wait()
        for_peers(lambda k: away(g, k).wait_send())
        for_peers(lambda k: back(g, k).wait())


def restore_kernel(owners, values_ref, unmix_ref, place_ref, out_ref, slots_s):
    energy = pl.program_id(0)
    width = out_ref.shape[2]
    share = out_ref.shape[1] // owners

    @pl.when(energy == 0)
    def _():
        unmix = unmix_ref[...]
        for r in range(share):
            slots_s[r] = dot(unmix, values_ref[:, r * width : (r + 1) * width]).astype(BF16)

    at = pl.ds(pl.multiple_of(energy * owners, owners), owners)
    ordered = jnp.concatenate([slots_s[r, at, :] for r in range(share)], axis=0)
    out_ref[0] = dot(place_ref[...], ordered)


def whole(shape):
    return pl.BlockSpec(shape, lambda e: (0,) * len(shape))


def per_energy(*shape):
    return pl.BlockSpec((1,) + shape, lambda e: (e,) + (0,) * len(shape))


def params():
    return pltpu.CompilerParams(dimension_semantics=("arbitrary",))


def cost(flops, moved):
    return pl.CostEstimate(flops=int(flops), bytes_accessed=int(moved), transcendentals=0)


def on_device(owners, green0, coupling, pattern, broaden, screened, order):
    here = green0.shape[0]
    size = green0.shape[-1]
    points = screened.shape[0]
    share = size // owners
    width = 2 * size
    flat = share * width
    green = green0.reshape(here, 2 * size, size)
    gamma = broaden.reshape(here, size, size)
    tile_size = size // pattern.shape[-1]
    spread = jnp.repeat(jnp.repeat(pattern[0], tile_size, axis=0), tile_size, axis=1)
    couple = coupling[0] * spread.astype(BF16)
    first = (lax.axis_index("space") == 0).astype(jnp.int32).reshape(1)
    by_row = order.reshape(owners, share).T.reshape(-1)
    ids = jnp.arange(size, dtype=jnp.int32)
    pick = (by_row[:, None] == ids[None, :]).astype(BF16)
    place = (by_row[None, :] == ids[:, None]).astype(BF16)

    ticks = np.arange(points)
    angles = (ticks[:, None] * ticks[None, :] % points) * (2.0 * math.pi / points)
    exact = np.concatenate([np.cos(angles), -np.sin(angles)], axis=1)
    high = exact.astype(BF16)
    low = (exact - high.astype(np.float64)).astype(BF16)
    table = jnp.asarray(np.concatenate([high, low], axis=0))
    where = np.arange(here * owners)
    source = (where % here) * owners + where // here
    mix_np = (source[:, None] == where[None, :]).astype(np.float32)
    mix = jnp.asarray(mix_np.astype(BF16))
    unmix = jnp.asarray(mix_np.T.astype(BF16))

    smem = pl.BlockSpec(memory_space=pltpu.SMEM)
    cell = (2 * size, size)
    work = 2.0 * here * size**3
    send, mult, base = pl.pallas_call(
        born_kernel,
        grid=(here,),
        in_specs=[smem, per_energy(*cell), whole((size, size))],
        out_specs=[per_energy(size, width), per_energy(*cell), per_energy(*cell)],
        out_shape=[
            jax.ShapeDtypeStruct((here, size, width), BF16),
            jax.ShapeDtypeStruct((here,) + cell, BF16),
            jax.ShapeDtypeStruct((here,) + cell, F32),
        ],
        compiler_params=params(),
        cost_estimate=cost(10 * work, 10 * here * 2 * size * size),
        name="born",
    )(first, green, couple)
    got = lax.ppermute(send, "space", [(0, 1), (1, 0)])
    mixed = pl.pallas_call(
        functools.partial(lesser_kernel, owners),
        grid=(here,),
        in_specs=[
            smem,
            per_energy(*cell),
            per_energy(size, width),
            per_energy(*cell),
            per_energy(size, size),
            whole((size, size)),
            whole((here * owners, here * owners)),
        ],
        out_specs=whole((here * owners, flat)),
        out_shape=jax.ShapeDtypeStruct((here * owners, flat), BF16),
        scratch_shapes=[
            pltpu.VMEM(cell, BF16),
            pltpu.VMEM((share, here * owners, width), BF16),
        ],
        compiler_params=params(),
        cost_estimate=cost(16 * work, 14 * here * 2 * size * size),
        name="lesser",
    )(first, mult, got, base, gamma, pick, mix)
    groups = max(parts for parts in range(1, 5) if share % parts == 0)
    anywhere = pl.BlockSpec(memory_space=pl.ANY)
    each_way = pltpu.SemaphoreType.DMA((groups, owners - 1))
    returned = pl.pallas_call(
        functools.partial(exchange_kernel, owners, groups, 1.0 / (points * math.sqrt(points))),
        in_specs=[pl.BlockSpec(memory_space=pltpu.VMEM), anywhere, anywhere],
        out_specs=anywhere,
        out_shape=jax.ShapeDtypeStruct((owners, here, flat), BF16),
        scratch_shapes=[
            pltpu.VMEM((points, share, width), F32),
            pltpu.VMEM((points, flat), F32),
            pltpu.VMEM((owners, here, flat), BF16),
            pltpu.VMEM((owners, here, flat), BF16),
            each_way,
            each_way,
            each_way,
            each_way,
            pltpu.SemaphoreType.DMA((2 + groups,)),
        ],
        compiler_params=pltpu.CompilerParams(collective_id=0, has_side_effects=True),
        name="exchange",
    )(table, mixed.reshape(owners, here, flat), screened.reshape(points, share, width))
    returned = returned.reshape(points, flat)
    out = pl.pallas_call(
        functools.partial(restore_kernel, owners),
        grid=(here,),
        in_specs=[
            whole((here * owners, flat)),
            whole((here * owners, here * owners)),
            whole((size, size)),
        ],
        out_specs=per_energy(size, width),
        out_shape=jax.ShapeDtypeStruct((here, size, width), F32),
        scratch_shapes=[pltpu.VMEM((share, here * owners, width), BF16)],
        compiler_params=params(),
        cost_estimate=cost(4 * work, 6 * points * flat),
        name="restore",
    )(returned, unmix, place)
    return out[:, None]


def solution(mesh):
    return jax.shard_map(
        functools.partial(on_device, mesh.shape["energy"]),
        mesh=mesh,
        in_specs=(
            P("energy", "space", None, None, None),
            P("space", None, None),
            P("space", None, None),
            P("energy", "space", None, None),
            P(None, "space", "energy", None),
            P(),
        ),
        out_specs=P("energy", "space", None, None),
        check_vma=False,
    )
```

```python
import functools
import math

import jax
import jax.numpy as jnp
import numpy as np
from jax import lax
from jax.experimental import pallas as pl
from jax.experimental.pallas import tpu as pltpu
from jax.sharding import PartitionSpec as P

F32 = jnp.float32
BF16 = jnp.bfloat16
PLAIN = ((1,), (0,))
LAST = ((1,), (1,))
FIRST = ((0,), (0,))


def dot(a, b, dims=PLAIN):
    return lax.dot_general(a, b, (dims, ((), ())), preferred_element_type=F32)


def complex_dot(left, right_re, right_im, dims=PLAIN):
    rows = left.shape[0] // 2
    with_re = dot(left, right_re, dims)
    with_im = dot(left, right_im, dims)
    return (with_re[:rows] - with_im[rows:], with_im[:rows] + with_re[rows:])


def stack(pair):
    return jnp.concatenate(pair, axis=0)


def born_kernel(first_ref, pattern_ref, green_ref, coupling_ref, send_ref, mult_ref, base_ref, couple_s):
    many, both, size = green_ref.shape
    rows = both // 2
    batch = range(many)

    @pl.when(pl.program_id(0) == 0)
    def _():
        tiles = pattern_ref.shape[0]
        tile_size = size // tiles
        lane = lax.broadcasted_iota(jnp.int32, (tile_size, size), 1)
        for i in range(tiles):
            keep = jnp.zeros((tile_size, size), F32)
            for j in range(tiles):
                inside = (lane >= j * tile_size) & (lane < (j + 1) * tile_size)
                keep = jnp.where(inside, pattern_ref[i, j].astype(F32), keep)
            at = slice(i * tile_size, (i + 1) * tile_size)
            couple_s[at, :] = (coupling_ref[at, :].astype(F32) * keep).astype(BF16)

    couple = couple_s[...]
    green = [green_ref[i] for i in batch]
    factor = [dot(g, couple).astype(BF16) for g in green]

    @pl.when(first_ref[0] == 1)
    def _():
        moved = [
            stack(complex_dot(f, g[:rows], g[rows:])).astype(BF16) for f, g in zip(factor, green)
        ]
        for i in batch:
            re, im = complex_dot(moved[i], factor[i][:rows], factor[i][rows:], LAST)
            re = green[i][:rows].astype(F32) + re
            im = green[i][rows:].astype(F32) + im
            base_ref[i, :rows] = re
            base_ref[i, rows:] = im
            send_ref[i] = jnp.concatenate([re, im], axis=1).astype(BF16)
            mult_ref[i] = green[i]

    @pl.when(first_ref[0] == 0)
    def _():
        for i in batch:
            base_ref[i] = green[i].astype(F32)
            added = [dot(factor[i][:rows], couple, FIRST), dot(factor[i][rows:], couple, FIRST)]
            send_ref[i] = jnp.concatenate(added, axis=1).astype(BF16)
            mult_ref[i] = factor[i]


def lesser_kernel(
    owners, first_ref, mult_ref, got_ref, base_ref, gamma_ref, pick_ref, mix_ref, out_ref, full_s, slots_s
):
    step = pl.program_id(0)
    many, both, size = mult_ref.shape
    rows = both // 2
    batch = range(many)
    mult = [mult_ref[i] for i in batch]
    moved = [
        stack(complex_dot(mult[i], got_ref[i, :, :rows], got_ref[i, :, rows:])).astype(BF16)
        for i in batch
    ]

    def finish(dims):
        for i in batch:
            extra = stack(complex_dot(moved[i], mult[i][:rows], mult[i][rows:], dims))
            full_s[i] = (base_ref[i] + extra).astype(BF16)

    @pl.when(first_ref[0] == 1)
    def _():
        finish(PLAIN)

    @pl.when(first_ref[0] == 0)
    def _():
        finish(LAST)

    full = [full_s[i] for i in batch]
    pick = pick_ref[...]
    weighted = [dot(full[i], gamma_ref[i]).astype(BF16) for i in batch]
    weighted = [stack((dot(pick, w[:rows]), dot(pick, w[rows:]))).astype(BF16) for w in weighted]
    share = rows // owners
    for i in batch:
        with_re = dot(weighted[i], full[i][:rows], LAST)
        with_im = dot(weighted[i], full[i][rows:], LAST)
        lesser = jnp.concatenate(
            [with_im[:rows] - with_re[rows:], with_re[:rows] + with_im[rows:]], axis=1
        ).astype(BF16)
        at = pl.ds(pl.multiple_of((step * many + i) * owners, owners), owners)
        for r in range(share):
            slots_s[r, at, :] = lesser[r * owners : (r + 1) * owners]

    @pl.when(step == pl.num_programs(0) - 1)
    def _():
        mix = mix_ref[...]
        width = 2 * size
        for r in range(share):
            out_ref[:, r * width : (r + 1) * width] = dot(mix, slots_s[r]).astype(BF16)


def times_i(values):
    half = values.shape[1] // 2
    return jnp.concatenate([-values[:, half:], values[:, :half]], axis=1)


def transform(table, upper, lower):
    both = dot(table, jnp.concatenate([upper, lower], axis=0).astype(BF16))
    points = upper.shape[0]
    return both[:points] + both[points:]


def exchange_kernel(
    owners,
    groups,
    scale,
    table_ref,
    mixed_ref,
    screened_ref,
    back_ref,
    screened_s,
    spectrum_s,
    got_s,
    sigma_s,
    away_sent,
    away_landed,
    back_sent,
    back_landed,
    own_sem,
):
    me = lax.axis_index("energy")
    points, share, width = screened_s.shape
    each = share // groups
    span = each * width

    def columns(g):
        return pl.ds(g * span, span)

    def away(g, k):
        peer = lax.rem(me + k, owners)
        return pltpu.make_async_remote_copy(
            src_ref=mixed_ref.at[peer, :, columns(g)],
            dst_ref=got_s.at[me, :, columns(g)],
            send_sem=away_sent.at[g, k - 1],
            recv_sem=away_landed.at[g, k - 1],
            device_id={"energy": peer},
            device_id_type=pl.DeviceIdType.MESH,
        )

    def back(g, k):
        peer = lax.rem(me + k, owners)
        return pltpu.make_async_remote_copy(
            src_ref=sigma_s.at[peer, :, columns(g)],
            dst_ref=back_ref.at[me, :, columns(g)],
            send_sem=back_sent.at[g, k - 1],
            recv_sem=back_landed.at[g, k - 1],
            device_id={"energy": peer},
            device_id_type=pl.DeviceIdType.MESH,
        )

    def for_peers(action):
        lax.fori_loop(1, owners, lambda k, c: (action(k), c)[1], 0)

    barrier = pltpu.get_barrier_semaphore()
    for_peers(
        lambda k: pl.semaphore_signal(
            barrier,
            inc=1,
            device_id={"energy": lax.rem(me + k, owners)},
            device_id_type=pl.DeviceIdType.MESH,
        )
    )
    load = pltpu.make_async_copy(screened_ref, screened_s, own_sem.at[0])
    load.start()
    keep = pltpu.make_async_copy(mixed_ref.at[me], got_s.at[me], own_sem.at[1])
    keep.start()
    pl.semaphore_wait(barrier, owners - 1)
    for g in range(groups):
        for_peers(lambda k: away(g, k).start())
    load.wait()
    table = table_ref[...]
    for r in range(share):
        values = screened_s[:, r, :]
        spectrum_s[:, r * width : (r + 1) * width] = transform(table, values, times_i(values)) * scale
    keep.wait()
    half = width // 2
    owns = []
    for g in range(groups):
        for_peers(lambda k: away(g, k).wait_recv())
        for r in range(g * each, (g + 1) * each):
            at = slice(r * width, (r + 1) * width)
            values = got_s[:, :, at].astype(F32).reshape(points, width)
            kernel = spectrum_s[:, at]
            spectrum = transform(table, values, times_i(values))
            kernel_re = jnp.concatenate([kernel[:, :half], kernel[:, :half]], axis=1)
            kernel_im = jnp.concatenate([kernel[:, half:], kernel[:, half:]], axis=1)
            product = spectrum * kernel_re + times_i(spectrum) * kernel_im
            result = transform(table, times_i(product), product)
            sigma_s[:, :, at] = result.reshape(owners, points // owners, width).astype(BF16)
        for_peers(lambda k: back(g, k).start())
        own = pltpu.make_async_copy(
            sigma_s.at[me, :, columns(g)], back_ref.at[me, :, columns(g)], own_sem.at[2 + g]
        )
        own.start()
        owns.append(own)
    for g in range(groups):
        owns[g].wait()
        for_peers(lambda k: away(g, k).wait_send())
        for_peers(lambda k: back(g, k).wait())


def restore_kernel(owners, values_ref, unmix_ref, place_ref, out_ref, slots_s):
    step = pl.program_id(0)
    many, size, width = out_ref.shape
    share = size // owners

    @pl.when(step == 0)
    def _():
        unmix = unmix_ref[...]
        for r in range(share):
            slots_s[r] = dot(unmix, values_ref[:, r * width : (r + 1) * width]).astype(BF16)

    for i in range(many):
        at = pl.ds(pl.multiple_of((step * many + i) * owners, owners), owners)
        ordered = jnp.concatenate([slots_s[r, at, :] for r in range(share)], axis=0)
        out_ref[i] = dot(place_ref[...], ordered)


def whole(shape):
    return pl.BlockSpec(shape, lambda e: (0,) * len(shape))


def energies(many, *shape):
    return pl.BlockSpec((many,) + shape, lambda e: (e,) + (0,) * len(shape))


def params():
    return pltpu.CompilerParams(dimension_semantics=("arbitrary",))


def cost(flops, moved):
    return pl.CostEstimate(flops=int(flops), bytes_accessed=int(moved), transcendentals=0)


def on_device(owners, green0, coupling, pattern, broaden, screened, order):
    here = green0.shape[0]
    size = green0.shape[-1]
    points = screened.shape[0]
    share = size // owners
    width = 2 * size
    flat = share * width
    green = green0.reshape(here, 2 * size, size)
    gamma = broaden.reshape(here, size, size)
    many = max(count for count in (1, 2, 4) if here % count == 0)
    first = (lax.axis_index("space") == 0).astype(jnp.int32).reshape(1)
    by_row = order.reshape(owners, share).T.reshape(-1)
    ids = jnp.arange(size, dtype=jnp.int32)
    pick = (by_row[:, None] == ids[None, :]).astype(BF16)
    place = (by_row[None, :] == ids[:, None]).astype(BF16)

    ticks = np.arange(points)
    angles = (ticks[:, None] * ticks[None, :] % points) * (2.0 * math.pi / points)
    exact = np.concatenate([np.cos(angles), -np.sin(angles)], axis=1)
    high = exact.astype(BF16)
    low = (exact - high.astype(np.float64)).astype(BF16)
    table = jnp.asarray(np.concatenate([high, low], axis=0))
    where = np.arange(here * owners)
    source = (where % here) * owners + where // here
    mix_np = (source[:, None] == where[None, :]).astype(np.float32)
    mix = jnp.asarray(mix_np.astype(BF16))
    unmix = jnp.asarray(mix_np.T.astype(BF16))

    smem = pl.BlockSpec(memory_space=pltpu.SMEM)
    cell = (2 * size, size)
    work = 2.0 * here * size**3
    send, mult, base = pl.pallas_call(
        born_kernel,
        grid=(here // many,),
        in_specs=[smem, smem, energies(many, *cell), whole((size, size))],
        out_specs=[energies(many, size, width), energies(many, *cell), energies(many, *cell)],
        out_shape=[
            jax.ShapeDtypeStruct((here, size, width), BF16),
            jax.ShapeDtypeStruct((here,) + cell, BF16),
            jax.ShapeDtypeStruct((here,) + cell, F32),
        ],
        scratch_shapes=[pltpu.VMEM((size, size), BF16)],
        compiler_params=params(),
        cost_estimate=cost(10 * work, 10 * here * 2 * size * size),
        name="born",
    )(first, pattern[0], green, coupling[0])
    got = lax.ppermute(send, "space", [(0, 1), (1, 0)])
    mixed = pl.pallas_call(
        functools.partial(lesser_kernel, owners),
        grid=(here // many,),
        in_specs=[
            smem,
            energies(many, *cell),
            energies(many, size, width),
            energies(many, *cell),
            energies(many, size, size),
            whole((size, size)),
            whole((here * owners, here * owners)),
        ],
        out_specs=whole((here * owners, flat)),
        out_shape=jax.ShapeDtypeStruct((here * owners, flat), BF16),
        scratch_shapes=[
            pltpu.VMEM((many,) + cell, BF16),
            pltpu.VMEM((share, here * owners, width), BF16),
        ],
        compiler_params=params(),
        cost_estimate=cost(16 * work, 14 * here * 2 * size * size),
        name="lesser",
    )(first, mult, got, base, gamma, pick, mix)
    groups = max(parts for parts in range(1, 5) if share % parts == 0)
    anywhere = pl.BlockSpec(memory_space=pl.ANY)
    each_way = pltpu.SemaphoreType.DMA((groups, owners - 1))
    returned = pl.pallas_call(
        functools.partial(exchange_kernel, owners, groups, 1.0 / (points * math.sqrt(points))),
        in_specs=[pl.BlockSpec(memory_space=pltpu.VMEM), anywhere, anywhere],
        out_specs=anywhere,
        out_shape=jax.ShapeDtypeStruct((owners, here, flat), BF16),
        scratch_shapes=[
            pltpu.VMEM((points, share, width), F32),
            pltpu.VMEM((points, flat), F32),
            pltpu.VMEM((owners, here, flat), BF16),
            pltpu.VMEM((owners, here, flat), BF16),
            each_way,
            each_way,
            each_way,
            each_way,
            pltpu.SemaphoreType.DMA((2 + groups,)),
        ],
        compiler_params=pltpu.CompilerParams(collective_id=0, has_side_effects=True),
        name="exchange",
    )(table, mixed.reshape(owners, here, flat), screened.reshape(points, share, width))
    returned = returned.reshape(points, flat)
    out = pl.pallas_call(
        functools.partial(restore_kernel, owners),
        grid=(here // many,),
        in_specs=[
            whole((here * owners, flat)),
            whole((here * owners, here * owners)),
            whole((size, size)),
        ],
        out_specs=energies(many, size, width),
        out_shape=jax.ShapeDtypeStruct((here, size, width), F32),
        scratch_shapes=[pltpu.VMEM((share, here * owners, width), BF16)],
        compiler_params=params(),
        cost_estimate=cost(4 * work, 6 * points * flat),
        name="restore",
    )(returned, unmix, place)
    return out[:, None]


def solution(mesh):
    return jax.shard_map(
        functools.partial(on_device, mesh.shape["energy"]),
        mesh=mesh,
        in_specs=(
            P("energy", "space", None, None, None),
            P("space", None, None),
            P("space", None, None),
            P("energy", "space", None, None),
            P(None, "space", "energy", None),
            P(),
        ),
        out_specs=P("energy", "space", None, None),
        check_vma=False,
    )
```

```python
import functools
import math

import jax
import jax.numpy as jnp
import numpy as np
from jax import lax
from jax.experimental import pallas as pl
from jax.experimental.pallas import tpu as pltpu
from jax.sharding import PartitionSpec as P

F32 = jnp.float32
BF16 = jnp.bfloat16
PLAIN = ((1,), (0,))
LAST = ((1,), (1,))
FIRST = ((0,), (0,))


def dot(a, b, dims=PLAIN):
    return lax.dot_general(a, b, (dims, ((), ())), preferred_element_type=F32)


def complex_dot(left, right_re, right_im, dims=PLAIN):
    rows = left.shape[0] // 2
    with_re = dot(left, right_re, dims)
    with_im = dot(left, right_im, dims)
    return (with_re[:rows] - with_im[rows:], with_im[:rows] + with_re[rows:])


def stack(pair):
    return jnp.concatenate(pair, axis=0)


def born_kernel(first_ref, pattern_ref, green_ref, coupling_ref, send_ref, mult_ref, base_ref, couple_s):
    many, both, size = green_ref.shape
    rows = both // 2
    batch = range(many)

    @pl.when(pl.program_id(0) == 0)
    def _():
        tiles = pattern_ref.shape[0]
        tile_size = size // tiles
        lane = lax.broadcasted_iota(jnp.int32, (tile_size, size), 1)
        for i in range(tiles):
            keep = jnp.zeros((tile_size, size), F32)
            for j in range(tiles):
                inside = (lane >= j * tile_size) & (lane < (j + 1) * tile_size)
                keep = jnp.where(inside, pattern_ref[i, j].astype(F32), keep)
            at = slice(i * tile_size, (i + 1) * tile_size)
            couple_s[at, :] = (coupling_ref[at, :].astype(F32) * keep).astype(BF16)

    couple = couple_s[...]
    green = [green_ref[i] for i in batch]
    factor = [dot(g, couple).astype(BF16) for g in green]

    @pl.when(first_ref[0] == 1)
    def _():
        moved = [
            stack(complex_dot(f, g[:rows], g[rows:])).astype(BF16) for f, g in zip(factor, green)
        ]
        for i in batch:
            re, im = complex_dot(moved[i], factor[i][:rows], factor[i][rows:], LAST)
            re = green[i][:rows].astype(F32) + re
            im = green[i][rows:].astype(F32) + im
            base_ref[i, :rows] = re
            base_ref[i, rows:] = im
            send_ref[i] = jnp.concatenate([re, im], axis=1).astype(BF16)
            mult_ref[i] = green[i]

    @pl.when(first_ref[0] == 0)
    def _():
        for i in batch:
            base_ref[i] = green[i].astype(F32)
            added = [dot(factor[i][:rows], couple, FIRST), dot(factor[i][rows:], couple, FIRST)]
            send_ref[i] = jnp.concatenate(added, axis=1).astype(BF16)
            mult_ref[i] = factor[i]


def lesser_kernel(
    owners, first_ref, mult_ref, got_ref, base_ref, gamma_ref, pick_ref, mix_ref, out_ref, full_s, slots_s
):
    step = pl.program_id(0)
    many, both, size = mult_ref.shape
    rows = both // 2
    batch = range(many)
    mult = [mult_ref[i] for i in batch]
    moved = [
        stack(complex_dot(mult[i], got_ref[i, :, :rows], got_ref[i, :, rows:])).astype(BF16)
        for i in batch
    ]

    def finish(dims):
        for i in batch:
            extra = stack(complex_dot(moved[i], mult[i][:rows], mult[i][rows:], dims))
            full_s[i] = (base_ref[i] + extra).astype(BF16)

    @pl.when(first_ref[0] == 1)
    def _():
        finish(PLAIN)

    @pl.when(first_ref[0] == 0)
    def _():
        finish(LAST)

    full = [full_s[i] for i in batch]
    pick = pick_ref[...]
    weighted = [dot(full[i], gamma_ref[i]).astype(BF16) for i in batch]
    weighted = [stack((dot(pick, w[:rows]), dot(pick, w[rows:]))).astype(BF16) for w in weighted]
    share = rows // owners
    for i in batch:
        with_re = dot(weighted[i], full[i][:rows], LAST)
        with_im = dot(weighted[i], full[i][rows:], LAST)
        lesser = jnp.concatenate(
            [with_im[:rows] - with_re[rows:], with_re[:rows] + with_im[rows:]], axis=1
        ).astype(BF16)
        at = pl.ds(pl.multiple_of((step * many + i) * owners, owners), owners)
        for r in range(share):
            slots_s[r, at, :] = lesser[r * owners : (r + 1) * owners]

    @pl.when(step == pl.num_programs(0) - 1)
    def _():
        mix = mix_ref[...]
        width = 2 * size
        for r in range(share):
            out_ref[:, r * width : (r + 1) * width] = dot(mix, slots_s[r]).astype(BF16)


def times_i(values):
    half = values.shape[1] // 2
    return jnp.concatenate([-values[:, half:], values[:, :half]], axis=1)


def transform(table, upper, lower):
    both = dot(table, jnp.concatenate([upper, lower], axis=0).astype(BF16))
    points = upper.shape[0]
    return both[:points] + both[points:]


def exchange_kernel(
    owners,
    groups,
    scale,
    table_ref,
    mixed_ref,
    screened_ref,
    back_ref,
    screened_s,
    spectrum_s,
    got_s,
    sigma_s,
    away_sent,
    away_landed,
    back_sent,
    back_landed,
    own_sem,
):
    me = lax.axis_index("energy")
    points, share, width = screened_s.shape
    each = share // groups
    span = each * width

    def columns(g):
        return pl.ds(g * span, span)

    def away(g, k):
        peer = lax.rem(me + k, owners)
        return pltpu.make_async_remote_copy(
            src_ref=mixed_ref.at[peer, :, columns(g)],
            dst_ref=got_s.at[me, :, columns(g)],
            send_sem=away_sent.at[g, k - 1],
            recv_sem=away_landed.at[g, k - 1],
            device_id={"energy": peer},
            device_id_type=pl.DeviceIdType.MESH,
        )

    def back(g, k):
        peer = lax.rem(me + k, owners)
        return pltpu.make_async_remote_copy(
            src_ref=sigma_s.at[peer, :, columns(g)],
            dst_ref=back_ref.at[me, :, columns(g)],
            send_sem=back_sent.at[g, k - 1],
            recv_sem=back_landed.at[g, k - 1],
            device_id={"energy": peer},
            device_id_type=pl.DeviceIdType.MESH,
        )

    def for_peers(action):
        lax.fori_loop(1, owners, lambda k, c: (action(k), c)[1], 0)

    barrier = pltpu.get_barrier_semaphore()
    for_peers(
        lambda k: pl.semaphore_signal(
            barrier,
            inc=1,
            device_id={"energy": lax.rem(me + k, owners)},
            device_id_type=pl.DeviceIdType.MESH,
        )
    )
    load = pltpu.make_async_copy(screened_ref, screened_s, own_sem.at[0])
    load.start()
    keep = pltpu.make_async_copy(mixed_ref.at[me], got_s.at[me], own_sem.at[1])
    keep.start()
    pl.semaphore_wait(barrier, owners - 1)
    for g in range(groups):
        for_peers(lambda k: away(g, k).start())
    load.wait()
    table = table_ref[...]
    for r in range(share):
        values = screened_s[:, r, :]
        spectrum_s[:, r * width : (r + 1) * width] = transform(table, values, times_i(values)) * scale
    keep.wait()
    half = width // 2
    owns = []
    for g in range(groups):
        for_peers(lambda k: away(g, k).wait_recv())
        for r in range(g * each, (g + 1) * each):
            at = slice(r * width, (r + 1) * width)
            values = got_s[:, :, at].astype(F32).reshape(points, width)
            kernel = spectrum_s[:, at]
            spectrum = transform(table, values, times_i(values))
            kernel_re = jnp.concatenate([kernel[:, :half], kernel[:, :half]], axis=1)
            kernel_im = jnp.concatenate([kernel[:, half:], kernel[:, half:]], axis=1)
            product = spectrum * kernel_re + times_i(spectrum) * kernel_im
            result = transform(table, times_i(product), product)
            sigma_s[:, :, at] = result.reshape(owners, points // owners, width).astype(BF16)
        for_peers(lambda k: back(g, k).start())
        own = pltpu.make_async_copy(
            sigma_s.at[me, :, columns(g)], back_ref.at[me, :, columns(g)], own_sem.at[2 + g]
        )
        own.start()
        owns.append(own)
    for g in range(groups):
        owns[g].wait()
        for_peers(lambda k: away(g, k).wait_send())
        for_peers(lambda k: back(g, k).wait())


def restore_kernel(owners, values_ref, unmix_ref, place_ref, out_ref, slots_s):
    step = pl.program_id(0)
    many, size, width = out_ref.shape
    share = size // owners

    @pl.when(step == 0)
    def _():
        unmix = unmix_ref[...]
        for r in range(share):
            slots_s[r] = dot(unmix, values_ref[:, r * width : (r + 1) * width]).astype(BF16)

    for i in range(many):
        at = pl.ds(pl.multiple_of((step * many + i) * owners, owners), owners)
        ordered = jnp.concatenate([slots_s[r, at, :] for r in range(share)], axis=0)
        out_ref[i] = dot(place_ref[...], ordered)


def whole(shape):
    return pl.BlockSpec(shape, lambda e: (0,) * len(shape))


def energies(many, *shape):
    return pl.BlockSpec((many,) + shape, lambda e: (e,) + (0,) * len(shape))


def params():
    return pltpu.CompilerParams(dimension_semantics=("arbitrary",))


def cost(flops, moved):
    return pl.CostEstimate(flops=int(flops), bytes_accessed=int(moved), transcendentals=0)


def on_device(owners, green0, coupling, pattern, broaden, screened, order):
    here = green0.shape[0]
    size = green0.shape[-1]
    points = screened.shape[0]
    share = size // owners
    width = 2 * size
    flat = share * width
    green = green0.reshape(here, 2 * size, size)
    gamma = broaden.reshape(here, size, size)
    many = max(count for count in (1, 2, 4) if here % count == 0)
    first = (lax.axis_index("space") == 0).astype(jnp.int32).reshape(1)
    by_row = order.reshape(owners, share).T.reshape(-1)
    ids = jnp.arange(size, dtype=jnp.int32)
    pick = (by_row[:, None] == ids[None, :]).astype(BF16)
    place = (by_row[None, :] == ids[:, None]).astype(BF16)

    ticks = np.arange(points)
    angles = (ticks[:, None] * ticks[None, :] % points) * (2.0 * math.pi / points)
    exact = np.concatenate([np.cos(angles), -np.sin(angles)], axis=1)
    high = exact.astype(BF16)
    low = (exact - high.astype(np.float64)).astype(BF16)
    table = jnp.asarray(np.concatenate([high, low], axis=0))
    where = np.arange(here * owners)
    source = (where % here) * owners + where // here
    mix_np = (source[:, None] == where[None, :]).astype(np.float32)
    mix = jnp.asarray(mix_np.astype(BF16))
    unmix = jnp.asarray(mix_np.T.astype(BF16))

    smem = pl.BlockSpec(memory_space=pltpu.SMEM)
    cell = (2 * size, size)
    work = 2.0 * here * size**3
    send, mult, base = pl.pallas_call(
        born_kernel,
        grid=(here // many,),
        in_specs=[smem, smem, energies(many, *cell), whole((size, size))],
        out_specs=[energies(many, size, width), energies(many, *cell), energies(many, *cell)],
        out_shape=[
            jax.ShapeDtypeStruct((here, size, width), BF16),
            jax.ShapeDtypeStruct((here,) + cell, BF16),
            jax.ShapeDtypeStruct((here,) + cell, F32),
        ],
        scratch_shapes=[pltpu.VMEM((size, size), BF16)],
        compiler_params=params(),
        cost_estimate=cost(10 * work, 10 * here * 2 * size * size),
        name="born",
    )(first, pattern[0], green, coupling[0])
    got = lax.ppermute(send, "space", [(0, 1), (1, 0)])
    mixed = pl.pallas_call(
        functools.partial(lesser_kernel, owners),
        grid=(here // many,),
        in_specs=[
            smem,
            energies(many, *cell),
            energies(many, size, width),
            energies(many, *cell),
            energies(many, size, size),
            whole((size, size)),
            whole((here * owners, here * owners)),
        ],
        out_specs=whole((here * owners, flat)),
        out_shape=jax.ShapeDtypeStruct((here * owners, flat), BF16),
        scratch_shapes=[
            pltpu.VMEM((many,) + cell, BF16),
            pltpu.VMEM((share, here * owners, width), BF16),
        ],
        compiler_params=params(),
        cost_estimate=cost(16 * work, 14 * here * 2 * size * size),
        name="lesser",
    )(first, mult, got, base, gamma, pick, mix)
    groups = max(parts for parts in range(1, 7) if share % parts == 0)
    anywhere = pl.BlockSpec(memory_space=pl.ANY)
    each_way = pltpu.SemaphoreType.DMA((groups, owners - 1))
    returned = pl.pallas_call(
        functools.partial(exchange_kernel, owners, groups, 1.0 / (points * math.sqrt(points))),
        in_specs=[pl.BlockSpec(memory_space=pltpu.VMEM), anywhere, anywhere],
        out_specs=anywhere,
        out_shape=jax.ShapeDtypeStruct((owners, here, flat), BF16),
        scratch_shapes=[
            pltpu.VMEM((points, share, width), F32),
            pltpu.VMEM((points, flat), F32),
            pltpu.VMEM((owners, here, flat), BF16),
            pltpu.VMEM((owners, here, flat), BF16),
            each_way,
            each_way,
            each_way,
            each_way,
            pltpu.SemaphoreType.DMA((2 + groups,)),
        ],
        compiler_params=pltpu.CompilerParams(collective_id=0, has_side_effects=True),
        name="exchange",
    )(table, mixed.reshape(owners, here, flat), screened.reshape(points, share, width))
    returned = returned.reshape(points, flat)
    out = pl.pallas_call(
        functools.partial(restore_kernel, owners),
        grid=(here // many,),
        in_specs=[
            whole((here * owners, flat)),
            whole((here * owners, here * owners)),
            whole((size, size)),
        ],
        out_specs=energies(many, size, width),
        out_shape=jax.ShapeDtypeStruct((here, size, width), F32),
        scratch_shapes=[pltpu.VMEM((share, here * owners, width), BF16)],
        compiler_params=params(),
        cost_estimate=cost(4 * work, 6 * points * flat),
        name="restore",
    )(returned, unmix, place)
    return out[:, None]


def solution(mesh):
    return jax.shard_map(
        functools.partial(on_device, mesh.shape["energy"]),
        mesh=mesh,
        in_specs=(
            P("energy", "space", None, None, None),
            P("space", None, None),
            P("space", None, None),
            P("energy", "space", None, None),
            P(None, "space", "energy", None),
            P(),
        ),
        out_specs=P("energy", "space", None, None),
        check_vma=False,
    )
```
